256 devices in a mesh: blk: 16 (over y, x_lo, core), head: 16 (over z, x_hi).
Axes of the slice: x: 4 (x_hi: 2, x_lo: 2; x = x_hi * 2 + x_lo), y: 4, z: 8, core: 2. Of those that a mesh axis runs over, the one named last changes fastest.
Arguments:
- queries: bfloat16 [32768, 2048], P(('blk', 'head')), may hold values from -6 to 6
- keys: bfloat16 [32768, 2048], P(('blk', 'head')), may hold values from -6 to 6
- values: bfloat16 [32768, 2048], P(('blk', 'head')), may hold values from -6 to 6
- slopes: float32 [16], replicated, may hold values from 0.02 to 0.4
- frames: int32 [32768], replicated, may hold values from 0 to 127, never falling along the last dimension, each value on 1 to 512 neighbouring positions
- block_list: int32 [16, 256, 32], replicated, may hold values from 0 to 255, as said below
Outputs:
- attended: bfloat16 [32768, 2048], P(('blk', 'head'))
The draws below stay inside these ranges and needn't reach their ends.
Inputs may be any that keep to these rules, and one draw needn't show every extreme that they name: `block_list`: each row lists 32 distinct block columns, among them the row's own block and the block 128 away, counted round.
All inputs are finite; a program needn't handle non-finite values.
Results may differ from the reference program's by a relative error of at most 0.0065.
Values may be sent and summed in bfloat16 or wider, within the bound.
A program may use at most 128 MiB of HBM per device.

```python
import math
import jax
import jax.numpy as jnp
import numpy as np
from jax import lax

HD = 128
HEADS = 16
BLOCK = 128
FRAME_MOST = 512
D = 2048
TOKENS = 32768
NB = 256
NNZ = 32
FRAMES = 128


def drawn_rows(key, salt):
    return jax.random.truncated_normal(jax.random.fold_in(key, salt), -6.0, 6.0, (TOKENS, D), jnp.float32)


def draw_queries(key, part):
    drawn = drawn_rows(key, 21)
    return drawn.astype(jnp.bfloat16)


def draw_keys(key, part):
    drawn = drawn_rows(key, 31)
    return drawn.astype(jnp.bfloat16)


def draw_block_list(key, part):
    rows_index = jnp.arange(NB, dtype=jnp.int32)
    frame_separation = jnp.abs(rows_index[:, None] - rows_index[None, :])
    reverse_sign = (rows_index[:, None] + NB // 2) % NB == rows_index[None, :]
    raw = jax.random.randint(jax.random.fold_in(key, 41), (HEADS, NB, NB), 0, 1 << 20, dtype=jnp.int32)
    block_ranking = raw // (1 + frame_separation)[None] * NB + rows_index[None, None, :]
    reward_boost = jnp.where((frame_separation == 0) | reverse_sign, 1 << 29, 0)
    block_ranking = block_ranking + reward_boost[None]
    picked = lax.top_k(block_ranking, NNZ)[1]
    return picked.astype(jnp.int32)


def level_of(key, shape, cuts, smallest, high):
    def one(axis_at, parts):
        heights = jax.random.uniform(jax.random.fold_in(jax.random.fold_in(key, 6), axis_at), (parts,), jnp.float32, smallest / len(cuts), high / len(cuts))
        return jnp.repeat(jnp.exp(heights), shape[axis_at] // parts).reshape((-1,) + (1,) * (len(shape) - axis_at - 1))

    factor_of = one(*cuts[0])
    for cut in cuts[1:]:
        factor_of = factor_of * one(*cut)
    return factor_of


def profile(amount, total, limit, skew):
    portions = [(1 << 20) // math.isqrt(standing ** skew) + 1 for standing in range(2, amount + 1)]
    rest, holding = total - limit - (amount - 1), [1] * (amount - 1)
    while rest > 0:
        candidates = [i for i in range(amount - 1) if holding[i] < limit]
        whole, remaining = sum([portions[i] for i in candidates]), rest
        for i in candidates:
            addition = min(limit - holding[i], max(1, remaining * portions[i] // whole), rest)
            holding[i] = holding[i] + addition
            rest = rest - addition
    return np.array([limit] + holding)


def ragged_sizes(rng, number_of, total, reach, lean):
    if number_of == 2:
        one = jax.random.randint(rng, (), max(1, total - reach), min(reach, total - 1) + 1)
        return jnp.stack([one, total - one])
    lengths = jnp.asarray(profile(number_of, total, reach, lean), jnp.int32)
    couples = (number_of - 1) // 2
    donor, receiver = lengths[1:1 + 2 * couples:2], lengths[2:2 + 2 * couples:2]
    slack = jnp.minimum(donor - 1, reach - receiver)
    moved = jax.random.randint(jax.random.fold_in(rng, 1), (couples,), 0, 1 << 20) % (slack + 1)
    lengths = lengths.at[1:1 + 2 * couples:2].set(donor - moved).at[2:2 + 2 * couples:2].set(receiver + moved)
    return lengths[jax.random.permutation(jax.random.fold_in(rng, 2), number_of)]


def gaussian(stream_key, shape, width, reach, shards=(), kind=jnp.bfloat16):
    level = level_of(stream_key, shape, shards, -0.22, 0.18) if shards else 1.0
    values = jax.random.normal(stream_key, shape, jnp.float32) * width * level
    return jnp.minimum(jnp.maximum(values, -reach), reach).astype(kind)


def setup_inputs(seed: int = 0) -> dict:
    streams_of = jax.random.split(jax.random.key(seed), 7)
    return {
        "queries": draw_queries(jax.random.fold_in(streams_of[6], 71), 0),
        "keys": draw_keys(jax.random.fold_in(streams_of[6], 71), 0),
        "values": gaussian(streams_of[2], (TOKENS, D), 1.0, 6.0, ((0, 256),)),
        "slopes": jnp.clip(jnp.exp(jax.random.uniform(streams_of[3], (HEADS,), jnp.float32, math.log(0.02), math.log(0.4))), 0.02, 0.4),
        "frames": jnp.searchsorted(jnp.cumsum(ragged_sizes(streams_of[4], FRAMES, TOKENS, FRAME_MOST, 0)), jnp.arange(TOKENS), side="right").astype(jnp.int32),
        "block_list": draw_block_list(jax.random.fold_in(streams_of[6], 71), 0),
    }


def attend_block(query_block, frame_block, columns, slope, key_head, value_head, frame_blocks):
    picked_keys = key_head[columns].reshape(-1, HD)
    picked_values = value_head[columns].reshape(-1, HD)
    picked_frames = frame_blocks[columns].reshape(-1)
    gap = jnp.abs(frame_block[:, None] - picked_frames[None, :]).astype(jnp.float32)
    block_scores = jnp.dot(query_block, picked_keys.T, preferred_element_type=jnp.float32) * (HD ** -0.5) - slope * gap
    largest = jnp.max(block_scores, axis=1)
    weights = jnp.exp(block_scores - largest[:, None])
    total = jnp.sum(weights, axis=1)
    summed = jnp.dot(weights.astype(jnp.bfloat16), picked_values, preferred_element_type=jnp.float32)
    return (summed / total[:, None]).astype(jnp.bfloat16)


def reference(queries, keys, values, slopes, frames, block_list):
    def split_heads(array):
        return array.reshape(NB, BLOCK, HEADS, HD).transpose(2, 0, 1, 3)

    query_heads = split_heads(queries)
    key_heads = split_heads(keys)
    value_heads = split_heads(values)
    frame_blocks = frames.reshape(NB, BLOCK)

    def one_head(packed):
        query_head, key_head, value_head, slope, lists = packed

        def one_block(index):
            return attend_block(query_head[index], frame_blocks[index], lists[index], slope, key_head, value_head, frame_blocks)

        return lax.map(one_block, jnp.arange(NB, dtype=jnp.int32))

    result = lax.map(one_head, (query_heads, key_heads, value_heads, slopes, block_list))
    return result.transpose(1, 2, 0, 3).reshape(TOKENS, HEADS * HD)
```

```python
import functools
import math

import jax
import jax.numpy as jnp
from jax import lax
from jax.experimental import pallas as pl
from jax.experimental.pallas import tpu as pltpu
from jax.sharding import PartitionSpec as P

HD = 128
HEADS = 16
BLOCK = 128
SCALE2 = HD**-0.5 * math.log2(math.e)


def attend(width, lists, query, key, value, frame_col, frame_row, out, scores):
    row = pl.program_id(0)
    q = query[...]
    mine = jnp.broadcast_to(frame_col[...], (BLOCK, BLOCK))
    top = None
    for slot in range(width):
        column = lists[row, slot]
        raw = lax.dot_general(q, key[column], (((1,), (1,)), ((), ())), preferred_element_type=jnp.float32)
        now = raw * SCALE2 - jnp.abs(mine - frame_row[column])
        scores[:, slot * BLOCK : (slot + 1) * BLOCK] = now
        top = now if top is None else jnp.maximum(top, now)
    top = jnp.broadcast_to(jnp.max(top, axis=1, keepdims=True), (BLOCK, BLOCK))
    total = jnp.zeros((BLOCK, BLOCK), jnp.float32)
    acc = jnp.zeros((BLOCK, HD), jnp.float32)
    for slot in range(0, width, 2):
        pair = []
        for part in (slot, slot + 1):
            w = jnp.exp2(scores[:, part * BLOCK : (part + 1) * BLOCK] - top)
            total = total + w
            pair.append(w.astype(jnp.bfloat16))
        both = jnp.concatenate([value[lists[row, slot]], value[lists[row, slot + 1]]], axis=0)
        acc = acc + jnp.dot(jnp.concatenate(pair, axis=1), both, preferred_element_type=jnp.float32)
    out[...] = (acc / jnp.sum(total, axis=1, keepdims=True)).astype(out.dtype)


def per_device(queries, keys, values, slopes, frames, block_list):
    query_group, key_group, value_group = (
        lax.all_to_all(a, "head", split_axis=1, concat_axis=0, tiled=True) for a in (queries, keys, values)
    )
    group_rows = query_group.shape[0]
    group_blocks = group_rows // BLOCK
    blocks = frames.shape[0] // BLOCK
    width = block_list.shape[2]
    start = lax.axis_index("blk") * group_blocks
    head = lax.axis_index("head")
    slope = lax.dynamic_slice_in_dim(slopes, head, 1) * math.log2(math.e)
    lists = lax.dynamic_slice(block_list, (head, start, 0), (1, group_blocks, width))[0]
    scaled = frames.astype(jnp.float32) * slope
    mine = lax.dynamic_slice_in_dim(scaled, start * BLOCK, group_rows).reshape(group_rows, 1)
    key_all = lax.all_gather(key_group, "blk", axis=0, tiled=True).reshape(blocks, BLOCK, HD)
    value_all = lax.all_gather(value_group, "blk", axis=0, tiled=True).reshape(blocks, BLOCK, HD)
    output = pl.pallas_call(
        functools.partial(attend, width),
        out_shape=jax.ShapeDtypeStruct((group_rows, HD), jnp.bfloat16),
        grid_spec=pltpu.PrefetchScalarGridSpec(
            num_scalar_prefetch=1,
            grid=(group_blocks,),
            in_specs=[
                pl.BlockSpec((BLOCK, HD), lambda i, t: (i, 0)),
                pl.BlockSpec((blocks, BLOCK, HD), lambda i, t: (0, 0, 0), pipeline_mode=pl.Buffered(1)),
                pl.BlockSpec((blocks, BLOCK, HD), lambda i, t: (0, 0, 0), pipeline_mode=pl.Buffered(1)),
                pl.BlockSpec((BLOCK, 1), lambda i, t: (i, 0)),
                pl.BlockSpec((blocks, 1, BLOCK), lambda i, t: (0, 0, 0), pipeline_mode=pl.Buffered(1)),
            ],
            out_specs=pl.BlockSpec((BLOCK, HD), lambda i, t: (i, 0)),
            scratch_shapes=[pltpu.VMEM((BLOCK, width * BLOCK), jnp.float32)],
        ),
        compiler_params=pltpu.CompilerParams(vmem_limit_bytes=48 << 20),
    )(lists, query_group, key_all, value_all, mine, scaled.reshape(blocks, 1, BLOCK))
    return lax.all_to_all(output, "head", split_axis=0, concat_axis=1, tiled=True)


def solution(mesh):
    rows = P(("blk", "head"), None)
    return jax.shard_map(
        per_device, mesh=mesh, in_specs=(rows, rows, rows, P(), P(), P()), out_specs=rows, check_vma=False
    )
```

```python
import functools
import math

import jax
import jax.numpy as jnp
from jax import lax
from jax.experimental import pallas as pl
from jax.experimental.pallas import tpu as pltpu
from jax.sharding import PartitionSpec as P

HD = 128
BLOCK = 128
LOG2E = math.log2(math.e)
SCALE2 = HD**-0.5 * LOG2E
Z = 8
PLANE = 16
TILES = 16
CHUNK = 4
MESH = pl.DeviceIdType.MESH


def offset_at(p):
    step = (p + 1) // 2
    return (Z + step * (2 * (p % 2) - 1)) % Z


PLACES = [0, 1, 3, 5, 7, 6, 4, 2]


def kernel(width, lists, rows, q_hbm, k_hbm, v_hbm, frame_col, frame_row, out,
           q_all, k_all, v_all, o_all, scores,
           local, send, scat, x_a, x_b, y_up, y_down, y_far, core_in, q_in, o_send, o_in):
    blk, head = lax.axis_index("blk"), lax.axis_index("head")
    z, xh = head // 2, head % 2
    xl, core = (blk // 2) % 2, blk % 2
    xp = blk + 2 - 4 * xl
    cp = blk + 1 - 2 * core
    yu, yd, yo = (blk + 4) % PLANE, (blk + 12) % PLANE, (blk + 8) % PLANE
    xpu, xpd, xpo = (xp + 4) % PLANE, (xp + 12) % PLANE, (xp + 8) % PLANE

    def peer(e, dz):
        return (xp if e else blk, ((z + dz) % Z) * 2 + (1 - xh if e else xh))

    peers = [peer(e, dz) for e in (0, 1) for dz in range(Z) if (e, dz) != (0, 0)]
    near = [(xp, head), (cp, head), (yu, head), (yd, head)]
    barrier = pltpu.get_barrier_semaphore()
    for d in peers + near:
        pl.semaphore_signal(barrier, inc=1, device_id=d, device_id_type=MESH)
    pl.semaphore_wait(barrier, len(peers) + len(near))

    def head_tile(ref, h):
        return ref.at[:, pl.ds(pl.multiple_of(h * HD, HD), HD)]

    def scatter(ref, dst, base_of, sem_of):
        for half in (0, 1):
            for e in (0, 1):
                for p in range(half * CHUNK, (half + 1) * CHUNK):
                    dz = (Z - offset_at(p)) % Z
                    if (e, dz) == (0, 0):
                        continue
                    to = peer(e, dz)
                    pltpu.make_async_remote_copy(
                        head_tile(ref, to[1]), dst.at[base_of(to[0]) + e * Z + p],
                        sem_of(None), sem_of(2 * half + e), device_id=to, device_id_type=MESH,
                    ).start()

    mine = blk * TILES
    own = [
        pltpu.make_async_copy(head_tile(ref, head), dst, local.at[n])
        for n, (ref, dst) in enumerate(((k_hbm, k_all.at[mine]), (v_hbm, v_all.at[mine]), (q_hbm, q_all.at[0])))
    ]
    for c in own:
        c.start()
    scatter(k_hbm, k_all, lambda b: b * TILES, lambda n: send.at[0] if n is None else scat.at[n])
    scatter(q_hbm, q_all, lambda b: 0, lambda n: send.at[2] if n is None else q_in.at[0])
    scatter(v_hbm, v_all, lambda b: b * TILES, lambda n: send.at[1] if n is None else scat.at[4 + n])

    def take(ref, start, tiles, sem):
        view = ref.at[pl.ds(start, tiles)]
        pltpu.make_async_copy(view, view, sem).wait()

    def gather(t, ref):
        def at(origin, ck):
            half, e = divmod(ck, 2)
            return origin * TILES + e * Z + half * CHUNK

        def push(start, tiles, to, sem):
            view = ref.at[pl.ds(start, tiles)]
            pltpu.make_async_remote_copy(
                view, view, send.at[t], sem, device_id=(to, head), device_id_type=MESH
            ).start()

        def to_core(start):
            push(start, CHUNK, cp, core_in.at[t])

        def begin(ck):
            s = at(blk, ck)
            if ck == 0:
                own[t].wait()
                take(ref, s + 1, CHUNK - 1, scat.at[4 * t + ck])
            else:
                take(ref, s, CHUNK, scat.at[4 * t + ck])
            first = ck % 2 == 0
            push(s, CHUNK, xp, x_a.at[2 * t + ck // 2] if first else x_b.at[8 * t + ck // 2 * 4])
            push(s, CHUNK, yu, y_up.at[6 * t + ck])
            push(s, CHUNK, yd, y_down.at[6 * t + ck])
            to_core(s)

        def across(ck):
            s = at(xp, ck)
            take(ref, s, CHUNK, x_a.at[2 * t + ck // 2])
            push(s, CHUNK, yu, y_up.at[6 * t + 4 + ck // 2])
            push(s, CHUNK, yd, y_down.at[6 * t + 4 + ck // 2])
            to_core(s)

        def along(ck, partner):
            n = 6 * t + (4 + ck // 2 if partner else ck)
            h = CHUNK // 2
            s = at(xpd if partner else yd, ck)
            take(ref, s, CHUNK, y_up.at[n])
            push(s, h, yu, y_far.at[n])
            if ck % 2:
                push(s, CHUNK, xp, x_b.at[8 * t + ck // 2 * 4 + 1])
            to_core(s)
            s = at(xpu if partner else yu, ck)
            take(ref, s, CHUNK, y_down.at[n])
            push(s + h, h, yd, y_far.at[n])
            if ck % 2:
                push(s, CHUNK, xp, x_b.at[8 * t + ck // 2 * 4 + 2])
            to_core(s)

        def far(ck, partner):
            n = 6 * t + (4 + ck // 2 if partner else ck)
            s = at(xpo if partner else yo, ck)
            take(ref, s, CHUNK, y_far.at[n])
            if ck % 2:
                push(s, CHUNK, xp, x_b.at[8 * t + ck // 2 * 4 + 3])
            to_core(s)

        def beside(ck, n):
            s = at((xp, xpd, xpu, xpo)[n], ck)
            take(ref, s, CHUNK, x_b.at[8 * t + ck // 2 * 4 + n])
            to_core(s)

        def finish():
            take(ref, 0, TILES * PLANE // 2, core_in.at[t])

        return [
            lambda: begin(0),
            lambda: begin(1),
            lambda: across(0),
            lambda: along(0, False),
            lambda: begin(2),
            lambda: along(1, False),
            lambda: beside(1, 0),
            lambda: along(0, True),
            lambda: begin(3),
            lambda: across(2),
            lambda: far(0, False),
            lambda: far(1, False),
            lambda: along(2, False),
            lambda: beside(1, 1),
            lambda: beside(1, 2),
            lambda: far(0, True),
            lambda: along(3, False),
            lambda: beside(3, 0),
            lambda: along(2, True),
            lambda: beside(1, 3),
            lambda: far(2, False),
            lambda: far(3, False),
            lambda: beside(3, 1),
            lambda: beside(3, 2),
            lambda: far(2, True),
            lambda: beside(3, 3),
            finish,
        ]

    for step in gather(0, k_all) + gather(1, v_all):
        step()
    own[2].wait()
    take(q_all, 1, TILES - 1, q_in.at[0])

    def home(i):
        e, dz = i // Z, offset_at(i % Z)
        to = ((z + dz) % Z) * 2 + (xh + e) % 2
        return (blk + e * (2 - 4 * xl), to)

    def block_row(j, carry):
        i = TILES - 1 - j
        q = q_all[i]
        here = jnp.broadcast_to(frame_col[pl.ds(pl.multiple_of(i * BLOCK, BLOCK), BLOCK), :], (BLOCK, BLOCK))
        top = None
        for slot in range(width):
            raw = lax.dot_general(
                q, k_all[lists[i, slot]], (((1,), (1,)), ((), ())), preferred_element_type=jnp.float32
            )
            now = raw * SCALE2 - jnp.abs(here - frame_row[rows[i, slot]])
            scores[:, slot * BLOCK : (slot + 1) * BLOCK] = now
            top = now if top is None else jnp.maximum(top, now)
        top = jnp.broadcast_to(jnp.max(top, axis=1, keepdims=True), (BLOCK, BLOCK))
        total = jnp.zeros((BLOCK, BLOCK), jnp.float32)
        acc = jnp.zeros((BLOCK, HD), jnp.float32)
        for slot in range(0, width, 2):
            pair = []
            for part in (slot, slot + 1):
                w = jnp.exp2(scores[:, part * BLOCK : (part + 1) * BLOCK] - top)
                total = total + w
                pair.append(w.astype(jnp.bfloat16))
            both = jnp.concatenate([v_all[lists[i, slot]], v_all[lists[i, slot + 1]]], axis=0)
            acc = acc + jnp.dot(jnp.concatenate(pair, axis=1), both, preferred_element_type=jnp.float32)
        o_all[i] = (acc / jnp.sum(total, axis=1, keepdims=True)).astype(o_all.dtype)

        @pl.when(i > 0)
        def _():
            pltpu.make_async_remote_copy(
                o_all.at[i], head_tile(out, head), o_send.at[0], o_in.at[0], device_id=home(i), device_id_type=MESH
            ).start()

        return carry

    lax.fori_loop(0, TILES, block_row, 0)
    last = pltpu.make_async_copy(o_all.at[0], head_tile(out, head), local.at[3])
    last.start()
    last.wait()
    take(o_all, 1, TILES - 1, o_in.at[0])
    take(o_all, 1, TILES - 1, o_send.at[0])
    take(q_all, 1, TILES - 1, send.at[2])
    for t, ref in ((0, k_all), (1, v_all)):
        take(ref, 0, 15 + 128 + 40 + 72, send.at[t])


def per_device(queries, keys, values, slopes, frames, block_list):
    width = block_list.shape[2]
    blocks = frames.shape[0] // BLOCK
    blk, head = lax.axis_index("blk"), lax.axis_index("head")
    z, xh = head // 2, head % 2
    slope = lax.dynamic_slice_in_dim(slopes, head, 1) * LOG2E
    scaled = frames.astype(jnp.float32) * slope

    def mine(array):
        parts = array.reshape(PLANE, Z, 2, -1)
        sources = (z + jnp.array([offset_at(p) for p in range(Z)])) % Z
        return jnp.concatenate(
            [
                lax.dynamic_slice(parts, (b, 0, x, 0), (1, Z, 1, parts.shape[3]))[0, :, 0][sources]
                for b, x in ((blk, xh), (blk ^ 2, 1 - xh))
            ]
        )

    rows = mine(lax.dynamic_index_in_dim(block_list, head, 0, keepdims=False))
    source_blk, source_z, source_x = rows // TILES, rows % TILES // 2, rows % 2
    column = source_x ^ xh
    place = jnp.array(PLACES)[(source_z - z) % Z]
    lists = (source_blk ^ (2 * column)) * TILES + column * Z + place
    frame_col = mine(scaled.reshape(blocks, BLOCK)).reshape(TILES * BLOCK, 1)
    frame_row = scaled.reshape(blocks, 1, BLOCK)
    smem, vmem = pl.BlockSpec(memory_space=pltpu.SMEM), pl.BlockSpec(memory_space=pltpu.VMEM)
    hbm = pl.BlockSpec(memory_space=pl.ANY)
    dma = pltpu.SemaphoreType.DMA
    return pl.pallas_call(
        functools.partial(kernel, width),
        out_shape=jax.ShapeDtypeStruct(queries.shape, jnp.bfloat16),
        in_specs=[smem, smem, hbm, hbm, hbm, vmem, vmem],
        out_specs=hbm,
        scratch_shapes=[
            pltpu.VMEM((TILES, BLOCK, HD), jnp.bfloat16),
            pltpu.VMEM((blocks, BLOCK, HD), jnp.bfloat16),
            pltpu.VMEM((blocks, BLOCK, HD), jnp.bfloat16),
            pltpu.VMEM((TILES, BLOCK, HD), jnp.bfloat16),
            pltpu.VMEM((BLOCK, width * BLOCK), jnp.float32),
            dma((4,)), dma((3,)), dma((8,)), dma((4,)), dma((16,)), dma((12,)), dma((12,)), dma((12,)),
            dma((2,)), dma((1,)), dma((1,)), dma((1,)),
        ],
        compiler_params=pltpu.CompilerParams(collective_id=0, has_side_effects=True, vmem_limit_bytes=56 << 20),
    )(lists, rows, queries, keys, values, frame_col, frame_row)


def solution(mesh):
    rows = P(("blk", "head"), None)
    return jax.shard_map(
        per_device, mesh=mesh, in_specs=(rows, rows, rows, P(), P(), P()), out_specs=rows, check_vma=False
    )
```

```python
import functools
import math

import jax
import jax.numpy as jnp
from jax import lax
from jax.experimental import pallas as pl
from jax.experimental.pallas import tpu as pltpu
from jax.sharding import PartitionSpec as P

HD = 128
BLOCK = 128
LOG2E = math.log2(math.e)
SCALE2 = HD**-0.5 * LOG2E
Z = 8
PLANE = 16
TILES = 16
CHUNK = 4
MESH = pl.DeviceIdType.MESH


def offset_at(p):
    step = (p + 1) // 2
    return (Z + step * (2 * (p % 2) - 1)) % Z


def place_of(dz):
    return jnp.where(dz <= Z // 2, jnp.maximum(2 * dz - 1, 0), 2 * (Z - dz))


def kernel(width, slopes, list_hbm, q_hbm, k_hbm, v_hbm, frame_hbm, out,
           rows, tiles_of, frame_row, here_all, q_all, k_all, v_all, o_all, scores, w_all, total_all,
           local, send, scat, x_a, x_b, y_up, y_down, y_far, core_in, q_in, o_send, o_in):
    blk, head = lax.axis_index("blk"), lax.axis_index("head")
    z, xh = head // 2, head % 2
    xl, core = (blk // 2) % 2, blk % 2
    xp = blk + 2 - 4 * xl
    cp = blk + 1 - 2 * core
    yu, yd, yo = (blk + 4) % PLANE, (blk + 12) % PLANE, (blk + 8) % PLANE
    xpu, xpd, xpo = (xp + 4) % PLANE, (xp + 12) % PLANE, (xp + 8) % PLANE

    def peer(e, dz):
        return (xp if e else blk, ((z + dz) % Z) * 2 + (1 - xh if e else xh))

    peers = [peer(e, dz) for e in (0, 1) for dz in range(Z) if (e, dz) != (0, 0)]
    near = [(xp, head), (cp, head), (yu, head), (yd, head)]
    barrier = pltpu.get_barrier_semaphore()
    for d in peers + near:
        pl.semaphore_signal(barrier, inc=1, device_id=d, device_id_type=MESH)
    pl.semaphore_wait(barrier, len(peers) + len(near))

    def head_tile(ref, h):
        return ref.at[:, pl.ds(pl.multiple_of(h * HD, HD), HD)]

    def scatter(ref, dst, base_of, sem_of):
        for half in (0, 1):
            for e in (0, 1):
                for p in range(half * CHUNK, (half + 1) * CHUNK):
                    dz = (Z - offset_at(p)) % Z
                    if (e, dz) == (0, 0):
                        continue
                    to = peer(e, dz)
                    pltpu.make_async_remote_copy(
                        head_tile(ref, to[1]), dst.at[base_of(to[0]) + e * Z + p],
                        sem_of(None), sem_of(2 * half + e), device_id=to, device_id_type=MESH,
                    ).start()

    mine = blk * TILES
    heads = rows.shape[1]
    pattern = [
        pltpu.make_async_copy(
            list_hbm.at[head, pl.ds(pl.multiple_of(b * heads, heads), heads)], rows.at[e], local.at[4 + e]
        )
        for e, b in ((0, blk), (1, xp))
    ]
    frame_copy = pltpu.make_async_copy(frame_hbm, frame_row, local.at[6])
    own = [
        pltpu.make_async_copy(head_tile(ref, head), dst, local.at[n])
        for n, (ref, dst) in enumerate(((k_hbm, k_all.at[mine]), (v_hbm, v_all.at[mine]), (q_hbm, q_all.at[0])))
    ]
    for c in own:
        c.start()
    scatter(k_hbm, k_all, lambda b: b * TILES, lambda n: send.at[0] if n is None else scat.at[n])
    scatter(q_hbm, q_all, lambda b: 0, lambda n: send.at[2] if n is None else q_in.at[0])
    scatter(v_hbm, v_all, lambda b: b * TILES, lambda n: send.at[1] if n is None else scat.at[4 + n])

    for c in pattern:
        c.start()
    frame_copy.start()

    def source(i):
        e = i // Z
        return e, (z + offset_at(i % Z)) % Z * 2 + (xh + e) % 2

    slope = slopes[head] * LOG2E
    frame_copy.wait()
    for c in pattern:
        c.wait()

    def query_frames(i, carry):
        e, row = source(i)
        line = frame_row[(blk + e * (2 - 4 * xl)) * heads + row].astype(jnp.float32) * slope
        here_all[i] = jnp.broadcast_to(line, (BLOCK, BLOCK)).T
        return carry

    lax.fori_loop(0, TILES, query_frames, 0)

    def take(ref, start, tiles, sem):
        view = ref.at[pl.ds(start, tiles)]
        pltpu.make_async_copy(view, view, sem).wait()

    def gather(t, ref):
        def at(origin, ck):
            half, e = divmod(ck, 2)
            return origin * TILES + e * Z + half * CHUNK

        def push(start, tiles, to, sem):
            view = ref.at[pl.ds(start, tiles)]
            pltpu.make_async_remote_copy(
                view, view, send.at[t], sem, device_id=(to, head), device_id_type=MESH
            ).start()

        def to_core(start):
            push(start, CHUNK, cp, core_in.at[t])

        def begin(ck):
            s = at(blk, ck)
            if ck == 0:
                own[t].wait()
                take(ref, s + 1, CHUNK - 1, scat.at[4 * t + ck])
            else:
                take(ref, s, CHUNK, scat.at[4 * t + ck])
            first = ck % 2 == 0
            push(s, CHUNK, xp, x_a.at[2 * t + ck // 2] if first else x_b.at[8 * t + ck // 2 * 4])
            push(s, CHUNK, yu, y_up.at[6 * t + ck])
            push(s, CHUNK, yd, y_down.at[6 * t + ck])
            to_core(s)

        def across(ck):
            s = at(xp, ck)
            take(ref, s, CHUNK, x_a.at[2 * t + ck // 2])
            push(s, CHUNK, yu, y_up.at[6 * t + 4 + ck // 2])
            push(s, CHUNK, yd, y_down.at[6 * t + 4 + ck // 2])
            to_core(s)

        def along(ck, partner):
            n = 6 * t + (4 + ck // 2 if partner else ck)
            h = CHUNK // 2
            s = at(xpd if partner else yd, ck)
            take(ref, s, CHUNK, y_up.at[n])
            push(s, h, yu, y_far.at[n])
            if ck % 2:
                push(s, CHUNK, xp, x_b.at[8 * t + ck // 2 * 4 + 1])
            to_core(s)
            s = at(xpu if partner else yu, ck)
            take(ref, s, CHUNK, y_down.at[n])
            push(s + h, h, yd, y_far.at[n])
            if ck % 2:
                push(s, CHUNK, xp, x_b.at[8 * t + ck // 2 * 4 + 2])
            to_core(s)

        def far(ck, partner):
            n = 6 * t + (4 + ck // 2 if partner else ck)
            s = at(xpo if partner else yo, ck)
            take(ref, s, CHUNK, y_far.at[n])
            if ck % 2:
                push(s, CHUNK, xp, x_b.at[8 * t + ck // 2 * 4 + 3])
            to_core(s)

        def beside(ck, n):
            s = at((xp, xpd, xpu, xpo)[n], ck)
            take(ref, s, CHUNK, x_b.at[8 * t + ck // 2 * 4 + n])
            to_core(s)

        def finish():
            take(ref, 0, TILES * PLANE // 2, core_in.at[t])

        return [
            lambda: begin(0),
            lambda: begin(1),
            lambda: across(0),
            lambda: along(0, False),
            lambda: begin(2),
            lambda: along(1, False),
            lambda: beside(1, 0),
            lambda: along(0, True),
            lambda: begin(3),
            lambda: across(2),
            lambda: far(0, False),
            lambda: far(1, False),
            lambda: along(2, False),
            lambda: beside(1, 1),
            lambda: beside(1, 2),
            lambda: far(0, True),
            lambda: along(3, False),
            lambda: beside(3, 0),
            lambda: along(2, True),
            lambda: beside(1, 3),
            lambda: far(2, False),
            lambda: far(3, False),
            lambda: beside(3, 1),
            lambda: beside(3, 2),
            lambda: far(2, True),
            lambda: beside(3, 3),
            finish,
        ]

    def weigh(i):
        e, row = source(i)
        q = q_all[i]
        here = here_all[i]
        top = None
        for slot in range(width):
            block = rows[e, row, slot]
            column = (block + xh) % 2
            group, dz = block // heads, (block % heads // 2 - z + Z) % Z
            tile = (group + column * (2 - group // 2 % 2 * 4)) * TILES + column * Z + place_of(dz)
            tiles_of[i, slot] = tile
            raw = lax.dot_general(q, k_all[tile], (((1,), (1,)), ((), ())), preferred_element_type=jnp.float32)
            now = raw * SCALE2 - jnp.abs(here - frame_row[block].astype(jnp.float32) * slope)
            scores[:, slot * BLOCK : (slot + 1) * BLOCK] = now
            top = now if top is None else jnp.maximum(top, now)
        top = jnp.broadcast_to(jnp.max(top, axis=1, keepdims=True), (BLOCK, BLOCK))
        total = jnp.zeros((BLOCK, BLOCK), jnp.float32)
        for slot in range(width):
            w = jnp.exp2(scores[:, slot * BLOCK : (slot + 1) * BLOCK] - top)
            total = total + w
            w_all[i, :, slot * BLOCK : (slot + 1) * BLOCK] = w.astype(w_all.dtype)
        total_all[i] = total

    key_steps, value_steps = gather(0, k_all), gather(1, v_all)
    early = 2
    for step in key_steps[:-5] + value_steps[:early] + key_steps[-5:]:
        step()
    own[2].wait()
    take(q_all, 1, TILES - 1, q_in.at[0])
    later = value_steps[early:]

    def weigh_and_pass(i, carry):
        weigh(i)
        for n in range(TILES):

            @pl.when(i == n)
            def _():
                for step in later[n * len(later) // TILES : (n + 1) * len(later) // TILES]:
                    step()

        return carry

    lax.fori_loop(0, TILES, weigh_and_pass, 0)

    def home(i):
        e, dz = i // Z, offset_at(i % Z)
        to = ((z + dz) % Z) * 2 + (xh + e) % 2
        return (blk + e * (2 - 4 * xl), to)

    def block_row(j, carry):
        i = TILES - 1 - j
        acc = jnp.zeros((BLOCK, HD), jnp.float32)
        for slot in range(0, width, 2):
            both = jnp.concatenate([v_all[tiles_of[i, slot]], v_all[tiles_of[i, slot + 1]]], axis=0)
            acc = acc + jnp.dot(
                w_all[i, :, slot * BLOCK : (slot + 2) * BLOCK], both, preferred_element_type=jnp.float32
            )
        o_all[i] = (acc / jnp.sum(total_all[i], axis=1, keepdims=True)).astype(o_all.dtype)

        @pl.when(i > 0)
        def _():
            pltpu.make_async_remote_copy(
                o_all.at[i], head_tile(out, head), o_send.at[0], o_in.at[0], device_id=home(i), device_id_type=MESH
            ).start()

        return carry

    lax.fori_loop(0, TILES, block_row, 0)
    last = pltpu.make_async_copy(o_all.at[0], head_tile(out, head), local.at[3])
    last.start()
    last.wait()
    take(o_all, 1, TILES - 1, o_in.at[0])
    take(o_all, 1, TILES - 1, o_send.at[0])
    take(q_all, 1, TILES - 1, send.at[2])
    for t, ref in ((0, k_all), (1, v_all)):
        take(ref, 0, 15 + 128 + 40 + 72, send.at[t])


def per_device(queries, keys, values, slopes, frames, block_list):
    heads, blocks, width = block_list.shape
    smem = pl.BlockSpec(memory_space=pltpu.SMEM)
    hbm = pl.BlockSpec(memory_space=pl.ANY)
    dma = pltpu.SemaphoreType.DMA
    return pl.pallas_call(
        functools.partial(kernel, width),
        out_shape=jax.ShapeDtypeStruct(queries.shape, jnp.bfloat16),
        in_specs=[smem, hbm, hbm, hbm, hbm, hbm],
        out_specs=hbm,
        scratch_shapes=[
            pltpu.SMEM((2, heads, width), jnp.int32),
            pltpu.SMEM((TILES, width), jnp.int32),
            pltpu.VMEM((blocks, 1, BLOCK), jnp.int32),
            pltpu.VMEM((TILES, BLOCK, BLOCK), jnp.float32),
            pltpu.VMEM((TILES, BLOCK, HD), jnp.bfloat16),
            pltpu.VMEM((blocks, BLOCK, HD), jnp.bfloat16),
            pltpu.VMEM((blocks, BLOCK, HD), jnp.bfloat16),
            pltpu.VMEM((TILES, BLOCK, HD), jnp.bfloat16),
            pltpu.VMEM((BLOCK, width * BLOCK), jnp.float32),
            pltpu.VMEM((TILES, BLOCK, width * BLOCK), jnp.bfloat16),
            pltpu.VMEM((TILES, BLOCK, BLOCK), jnp.float32),
            dma((7,)), dma((3,)), dma((8,)), dma((4,)), dma((16,)), dma((12,)), dma((12,)), dma((12,)),
            dma((2,)), dma((1,)), dma((1,)), dma((1,)),
        ],
        compiler_params=pltpu.CompilerParams(collective_id=0, has_side_effects=True, vmem_limit_bytes=56 << 20),
    )(slopes, block_list, queries, keys, values, frames.reshape(blocks, 1, BLOCK))


def solution(mesh):
    rows = P(("blk", "head"), None)
    return jax.shard_map(
        per_device, mesh=mesh, in_specs=(rows, rows, rows, P(), P(), P()), out_specs=rows, check_vma=False
    )
```

```python
import functools
import math

import jax
import jax.numpy as jnp
from jax import lax
from jax.experimental import pallas as pl
from jax.experimental.pallas import tpu as pltpu
from jax.sharding import PartitionSpec as P

HD = 128
BLOCK = 128
LANES = 128
LOG2E = math.log2(math.e)
SCALE2 = HD**-0.5 * LOG2E
Z = 8
PLANE = 16
TILES = 16
CHUNKS = [(0, 4), (9, 3), (4, 5), (12, 4)]
CROSS_FIRST = sum(tiles for _, tiles in CHUNKS[::2])
MESH = pl.DeviceIdType.MESH


def offset_at(p):
    step = (p + 1) // 2
    return (Z + step * (2 * (p % 2) - 1)) % Z


def place_of(dz):
    return jnp.where(dz <= Z // 2, jnp.maximum(2 * dz - 1, 0), 2 * (Z - dz))


def kernel(width, slopes, list_hbm, q_hbm, k_hbm, v_hbm, frame_hbm, out,
           rows, tiles_of, frame_row, here_all, q_all, k_all, v_all, o_all, scores, top_now, w_all, total_all,
           local, send, scat, x_a, x_b, y_up, y_down, y_far, core_in, q_in, o_send, o_in):
    blk, head = lax.axis_index("blk"), lax.axis_index("head")
    z, xh = head // 2, head % 2
    xl, core = (blk // 2) % 2, blk % 2
    xp = blk + 2 - 4 * xl
    cp = blk + 1 - 2 * core
    yu, yd, yo = (blk + 4) % PLANE, (blk + 12) % PLANE, (blk + 8) % PLANE
    xpu, xpd, xpo = (xp + 4) % PLANE, (xp + 12) % PLANE, (xp + 8) % PLANE

    def peer(e, dz):
        return (xp if e else blk, ((z + dz) % Z) * 2 + (1 - xh if e else xh))

    peers = [peer(e, dz) for e in (0, 1) for dz in range(Z) if (e, dz) != (0, 0)]
    near = [(xp, head), (cp, head), (yu, head), (yd, head)]
    barrier = pltpu.get_barrier_semaphore()
    for d in peers + near:
        pl.semaphore_signal(barrier, inc=1, device_id=d, device_id_type=MESH)
    pl.semaphore_wait(barrier, len(peers) + len(near))

    def head_tile(ref, h):
        return ref.at[:, pl.ds(pl.multiple_of(h * HD, HD), HD)]

    def scatter(ref, dst, base_of, sem_of):
        for ck, (first, tiles) in enumerate(CHUNKS):
            for n in range(first, first + tiles):
                e, p = divmod(n, Z)
                dz = (Z - offset_at(p)) % Z
                if (e, dz) == (0, 0):
                    continue
                to = peer(e, dz)
                pltpu.make_async_remote_copy(
                    head_tile(ref, to[1]), dst.at[base_of(to[0]) + n],
                    sem_of(None), sem_of(ck), device_id=to, device_id_type=MESH,
                ).start()

    mine = blk * TILES
    per = LANES // TILES
    pattern = pltpu.make_async_copy(
        list_hbm.at[head, :, pl.ds(pl.multiple_of(blk // per * LANES, LANES), LANES)], rows, local.at[4]
    )
    frame_copy = pltpu.make_async_copy(frame_hbm, frame_row, local.at[5])
    own = [
        pltpu.make_async_copy(head_tile(ref, head), dst, local.at[n])
        for n, (ref, dst) in enumerate(((k_hbm, k_all.at[mine]), (v_hbm, v_all.at[mine]), (q_hbm, q_all.at[0])))
    ]
    for c in own:
        c.start()
    scatter(k_hbm, k_all, lambda b: b * TILES, lambda n: send.at[0] if n is None else scat.at[n])
    scatter(q_hbm, q_all, lambda b: 0, lambda n: send.at[2] if n is None else q_in.at[0])
    scatter(v_hbm, v_all, lambda b: b * TILES, lambda n: send.at[1] if n is None else scat.at[4 + n])

    pattern.start()
    frame_copy.start()

    def source(i):
        e = i // Z
        return e, (z + offset_at(i % Z)) % Z * 2 + (xh + e) % 2

    slope = slopes[head] * LOG2E
    frame_copy.wait()
    pattern.wait()

    def query_frames(i, carry):
        e, row = source(i)
        line = frame_row[(blk + e * (2 - 4 * xl)) * TILES + row].astype(jnp.float32) * slope
        here_all[i] = jnp.broadcast_to(line, (BLOCK, BLOCK)).T
        return carry

    lax.fori_loop(0, TILES, query_frames, 0)

    def take(ref, start, tiles, sem):
        view = ref.at[pl.ds(start, tiles)]
        pltpu.make_async_copy(view, view, sem).wait()

    def gather(t, ref):
        def at(origin, ck):
            return origin * TILES + CHUNKS[ck][0]

        def push(start, tiles, to, sem):
            view = ref.at[pl.ds(start, tiles)]
            pltpu.make_async_remote_copy(
                view, view, send.at[t], sem, device_id=(to, head), device_id_type=MESH
            ).start()

        def to_core(start, ck):
            push(start, CHUNKS[ck][1], cp, core_in.at[t])

        def begin(ck):
            s = at(blk, ck)
            if ck == 0:
                own[t].wait()
                take(ref, s + 1, CHUNKS[ck][1] - 1, scat.at[4 * t + ck])
            else:
                take(ref, s, CHUNKS[ck][1], scat.at[4 * t + ck])
            first = ck % 2 == 0
            push(s, CHUNKS[ck][1], xp, x_a.at[2 * t + ck // 2] if first else x_b.at[8 * t + ck // 2 * 4])
            push(s, CHUNKS[ck][1], yu, y_up.at[6 * t + ck])
            push(s, CHUNKS[ck][1], yd, y_down.at[6 * t + ck])
            to_core(s, ck)

        def across(ck):
            s = at(xp, ck)
            take(ref, s, CHUNKS[ck][1], x_a.at[2 * t + ck // 2])
            push(s, CHUNKS[ck][1], yu, y_up.at[6 * t + 4 + ck // 2])
            push(s, CHUNKS[ck][1], yd, y_down.at[6 * t + 4 + ck // 2])
            to_core(s, ck)

        def along(ck, partner):
            n = 6 * t + (4 + ck // 2 if partner else ck)
            h = (CHUNKS[ck][1] + ck // 2) // 2
            s = at(xpd if partner else yd, ck)
            take(ref, s, CHUNKS[ck][1], y_up.at[n])
            push(s, h, yu, y_far.at[n])
            if ck % 2:
                push(s, CHUNKS[ck][1], xp, x_b.at[8 * t + ck // 2 * 4 + 1])
            to_core(s, ck)
            s = at(xpu if partner else yu, ck)
            take(ref, s, CHUNKS[ck][1], y_down.at[n])
            push(s + h, CHUNKS[ck][1] - h, yd, y_far.at[n])
            if ck % 2:
                push(s, CHUNKS[ck][1], xp, x_b.at[8 * t + ck // 2 * 4 + 2])
            to_core(s, ck)

        def far(ck, partner):
            n = 6 * t + (4 + ck // 2 if partner else ck)
            s = at(xpo if partner else yo, ck)
            take(ref, s, CHUNKS[ck][1], y_far.at[n])
            if ck % 2:
                push(s, CHUNKS[ck][1], xp, x_b.at[8 * t + ck // 2 * 4 + 3])
            to_core(s, ck)

        def beside(ck, n):
            s = at((xp, xpd, xpu, xpo)[n], ck)
            take(ref, s, CHUNKS[ck][1], x_b.at[8 * t + ck // 2 * 4 + n])
            to_core(s, ck)

        def finish():
            take(ref, 0, TILES * PLANE // 2, core_in.at[t])

        return begin, across, along, far, beside, finish

    def score(i):
        e, row = source(i)
        place = (blk + e * (2 - 4 * xl)) % per * TILES + row
        q = q_all[i]
        here = here_all[i]
        top = None
        for slot in range(width):
            block = rows[slot, place]
            column = (block + xh) % 2
            group, dz = block // TILES, (block % TILES // 2 - z + Z) % Z
            tile = (group + column * (2 - group // 2 % 2 * 4)) * TILES + column * Z + place_of(dz)
            tiles_of[i, slot] = tile
            raw = lax.dot_general(q, k_all[tile], (((1,), (1,)), ((), ())), preferred_element_type=jnp.float32)
            now = raw * SCALE2 - jnp.abs(here - frame_row[block].astype(jnp.float32) * slope)
            scores[:, slot * BLOCK : (slot + 1) * BLOCK] = now
            top = now if top is None else jnp.maximum(top, now)
        top_now[...] = jnp.broadcast_to(jnp.max(top, axis=1, keepdims=True), (BLOCK, BLOCK))

    def weigh(i):
        top = top_now[...]
        total = jnp.zeros((BLOCK, BLOCK), jnp.float32)
        for slot in range(width):
            w = jnp.exp2(scores[:, slot * BLOCK : (slot + 1) * BLOCK] - top)
            total = total + w
            w_all[i, :, slot * BLOCK : (slot + 1) * BLOCK] = w.astype(w_all.dtype)
        total_all[i] = total

    begin, across, along, far, beside, finish = gather(0, k_all)
    value_begin, value_across, value_along, value_far, value_beside, value_finish = gather(1, v_all)
    begin(0), begin(1), across(0), along(0, False), begin(2), along(1, False), beside(1, 0), along(0, True)
    begin(3), across(2), far(0, False), far(1, False), along(2, False), beside(1, 1), beside(1, 2), far(0, True)
    along(3, False), beside(3, 0), along(2, True), beside(1, 3), far(2, False), far(3, False)
    value_begin(0), value_begin(1)
    beside(3, 1), beside(3, 2), far(2, True), beside(3, 3), finish()
    own[2].wait()
    take(q_all, 1, TILES - 1, q_in.at[0])
    value_begin(2), value_begin(3)
    later = {
        1: [lambda: value_across(0), lambda: value_along(0, False)],
        3: [lambda: value_along(1, False)],
        5: [lambda: value_beside(1, 0)],
        7: [lambda: value_across(2), lambda: value_along(2, False)],
        10: [lambda: value_along(3, False)],
        12: [lambda: value_beside(3, 0)],
        14: [lambda: value_along(0, True)],
        15: [lambda: value_beside(1, 1)],
        16: [lambda: value_far(0, False)],
        17: [lambda: value_far(1, False)],
        18: [lambda: value_beside(1, 2)],
        20: [lambda: value_along(2, True)],
        21: [lambda: value_beside(3, 1)],
        23: [lambda: value_far(2, False)],
        24: [lambda: value_far(3, False)],
        25: [lambda: value_beside(3, 2)],
        27: [lambda: value_far(0, True)],
        28: [lambda: value_far(2, True)],
        29: [lambda: value_beside(1, 3)],
        31: [lambda: value_beside(3, 3)],
    }

    def pass_on(i, part):
        for half, steps in later.items():
            if half % 2 == part:

                @pl.when(i == half // 2)
                def _(steps=steps):
                    for step in steps:
                        step()

    def weigh_and_pass(i, carry):
        score(i)
        pass_on(i, 0)
        weigh(i)
        pass_on(i, 1)
        return carry

    lax.fori_loop(0, TILES, weigh_and_pass, 0)
    value_finish()

    def home(i):
        e, dz = i // Z, offset_at(i % Z)
        to = ((z + dz) % Z) * 2 + (xh + e) % 2
        return (blk + e * (2 - 4 * xl), to)

    def block_row(j, carry):
        i = TILES - 1 - j
        acc = jnp.zeros((BLOCK, HD), jnp.float32)
        for slot in range(0, width, 2):
            both = jnp.concatenate([v_all[tiles_of[i, slot]], v_all[tiles_of[i, slot + 1]]], axis=0)
            acc = acc + jnp.dot(
                w_all[i, :, slot * BLOCK : (slot + 2) * BLOCK], both, preferred_element_type=jnp.float32
            )
        o_all[i] = (acc / jnp.sum(total_all[i], axis=1, keepdims=True)).astype(o_all.dtype)

        @pl.when(i > 0)
        def _():
            pltpu.make_async_remote_copy(
                o_all.at[i], head_tile(out, head), o_send.at[0], o_in.at[0], device_id=home(i), device_id_type=MESH
            ).start()

        return carry

    lax.fori_loop(0, TILES, block_row, 0)
    last = pltpu.make_async_copy(o_all.at[0], head_tile(out, head), local.at[3])
    last.start()
    last.wait()
    take(o_all, 1, TILES - 1, o_in.at[0])
    take(o_all, 1, TILES - 1, o_send.at[0])
    take(q_all, 1, TILES - 1, send.at[2])
    for t, ref in ((0, k_all), (1, v_all)):
        take(ref, 0, 15 + 128 + (64 - 3 * CROSS_FIRST) + (48 + 3 * CROSS_FIRST), send.at[t])


def per_device(queries, keys, values, slopes, frames, block_list):
    blocks, width = block_list.shape[1:]
    smem = pl.BlockSpec(memory_space=pltpu.SMEM)
    hbm = pl.BlockSpec(memory_space=pl.ANY)
    dma = pltpu.SemaphoreType.DMA
    return pl.pallas_call(
        functools.partial(kernel, width),
        out_shape=jax.ShapeDtypeStruct(queries.shape, jnp.bfloat16),
        in_specs=[smem, hbm, hbm, hbm, hbm, hbm],
        out_specs=hbm,
        scratch_shapes=[
            pltpu.SMEM((width, LANES), jnp.int32),
            pltpu.SMEM((TILES, width), jnp.int32),
            pltpu.VMEM((blocks, 1, BLOCK), jnp.int32),
            pltpu.VMEM((TILES, BLOCK, BLOCK), jnp.float32),
            pltpu.VMEM((TILES, BLOCK, HD), jnp.bfloat16),
            pltpu.VMEM((blocks, BLOCK, HD), jnp.bfloat16),
            pltpu.VMEM((blocks, BLOCK, HD), jnp.bfloat16),
            pltpu.VMEM((TILES, BLOCK, HD), jnp.bfloat16),
            pltpu.VMEM((BLOCK, width * BLOCK), jnp.float32),
            pltpu.VMEM((BLOCK, BLOCK), jnp.float32),
            pltpu.VMEM((TILES, BLOCK, width * BLOCK), jnp.bfloat16),
            pltpu.VMEM((TILES, BLOCK, BLOCK), jnp.float32),
            dma((6,)), dma((3,)), dma((8,)), dma((4,)), dma((16,)), dma((12,)), dma((12,)), dma((12,)),
            dma((2,)), dma((1,)), dma((1,)), dma((1,)),
        ],
        compiler_params=pltpu.CompilerParams(collective_id=0, has_side_effects=True, vmem_limit_bytes=56 << 20),
    )(slopes, block_list.transpose(0, 2, 1), queries, keys, values, frames.reshape(blocks, 1, BLOCK))


def solution(mesh):
    rows = P(("blk", "head"), None)
    return jax.shard_map(
        per_device, mesh=mesh, in_specs=(rows, rows, rows, P(), P(), P()), out_specs=rows, check_vma=False
    )
```

```python
import functools
import math

import jax
import jax.numpy as jnp
from jax import lax
from jax.experimental import pallas as pl
from jax.experimental.pallas import tpu as pltpu
from jax.sharding import PartitionSpec as P

HD = 128
BLOCK = 128
LANES = 128
LOG2E = math.log2(math.e)
SCALE2 = HD**-0.5 * LOG2E
Z = 8
PLANE = 16
LATE = 3
TILES = 16
CHUNKS = [(0, 4), (9, 3), (4, 5), (12, 4)]
CROSS_FIRST = sum(tiles for _, tiles in CHUNKS[::2])
MESH = pl.DeviceIdType.MESH


def offset_at(p):
    step = (p + 1) // 2
    return (Z + step * (2 * (p % 2) - 1)) % Z


def place_of(dz):
    return jnp.where(dz <= Z // 2, jnp.maximum(2 * dz - 1, 0), 2 * (Z - dz))


def kernel(width, slopes, list_hbm, q_hbm, k_hbm, v_hbm, frame_hbm, out,
           rows, tiles_of, frame_row, here_all, q_all, k_all, v_all, o_all, scores, top_now, w_all, total_all,
           local, send, scat, x_a, x_b, y_up, y_down, y_far, core_in, q_in, o_send, o_in):
    blk, head = lax.axis_index("blk"), lax.axis_index("head")
    z, xh = head // 2, head % 2
    xl, core = (blk // 2) % 2, blk % 2
    xp = blk + 2 - 4 * xl
    cp = blk + 1 - 2 * core
    yu, yd, yo = (blk + 4) % PLANE, (blk + 12) % PLANE, (blk + 8) % PLANE
    xpu, xpd, xpo = (xp + 4) % PLANE, (xp + 12) % PLANE, (xp + 8) % PLANE

    def peer(e, dz):
        return (xp if e else blk, ((z + dz) % Z) * 2 + (1 - xh if e else xh))

    peers = [peer(e, dz) for e in (0, 1) for dz in range(Z) if (e, dz) != (0, 0)]
    near = [(xp, head), (cp, head), (yu, head), (yd, head)]
    barrier = pltpu.get_barrier_semaphore()
    for d in peers + near:
        pl.semaphore_signal(barrier, inc=1, device_id=d, device_id_type=MESH)
    pl.semaphore_wait(barrier, len(peers) + len(near))

    def head_tile(ref, h):
        return ref.at[:, pl.ds(pl.multiple_of(h * HD, HD), HD)]

    def scatter(ref, dst, base_of, sem_of):
        for ck, (first, tiles) in enumerate(CHUNKS):
            for n in range(first, first + tiles):
                e, p = divmod(n, Z)
                dz = (Z - offset_at(p)) % Z
                if (e, dz) == (0, 0):
                    continue
                to = peer(e, dz)
                pltpu.make_async_remote_copy(
                    head_tile(ref, to[1]), dst.at[base_of(to[0]) + n],
                    sem_of(None), sem_of(ck), device_id=to, device_id_type=MESH,
                ).start()

    mine = blk * TILES
    per = LANES // TILES
    pattern = pltpu.make_async_copy(
        list_hbm.at[head, :, pl.ds(pl.multiple_of(blk // per * LANES, LANES), LANES)], rows, local.at[4]
    )
    frame_copy = pltpu.make_async_copy(frame_hbm, frame_row, local.at[5])
    own = [
        pltpu.make_async_copy(head_tile(ref, head), dst, local.at[n])
        for n, (ref, dst) in enumerate(((k_hbm, k_all.at[mine]), (v_hbm, v_all.at[mine]), (q_hbm, q_all.at[0])))
    ]
    for c in own:
        c.start()
    scatter(k_hbm, k_all, lambda b: b * TILES, lambda n: send.at[0] if n is None else scat.at[n])
    scatter(q_hbm, q_all, lambda b: 0, lambda n: send.at[2] if n is None else q_in.at[0])
    scatter(v_hbm, v_all, lambda b: b * TILES, lambda n: send.at[1] if n is None else scat.at[4 + n])

    pattern.start()
    frame_copy.start()

    def source(i):
        e = i // Z
        return e, (z + offset_at(i % Z)) % Z * 2 + (xh + e) % 2

    slope = slopes[head] * LOG2E

    def query_frames(i, carry):
        e, row = source(i)
        line = frame_row[(blk + e * (2 - 4 * xl)) * TILES + row].astype(jnp.float32) * slope
        here_all[i] = jnp.broadcast_to(line, (BLOCK, BLOCK)).T
        return carry

    def take(ref, start, tiles, sem):
        view = ref.at[pl.ds(start, tiles)]
        pltpu.make_async_copy(view, view, sem).wait()

    def gather(t, ref):
        def at(origin, ck):
            return origin * TILES + CHUNKS[ck][0]

        def push(start, tiles, to, sem):
            view = ref.at[pl.ds(start, tiles)]
            pltpu.make_async_remote_copy(
                view, view, send.at[t], sem, device_id=(to, head), device_id_type=MESH
            ).start()

        def to_core(start, ck):
            push(start, CHUNKS[ck][1], cp, core_in.at[t])

        def begin(ck):
            s = at(blk, ck)
            if ck == 0:
                own[t].wait()
                take(ref, s + 1, CHUNKS[ck][1] - 1, scat.at[4 * t + ck])
            else:
                take(ref, s, CHUNKS[ck][1], scat.at[4 * t + ck])
            first = ck % 2 == 0
            push(s, CHUNKS[ck][1], xp, x_a.at[2 * t + ck // 2] if first else x_b.at[8 * t + ck // 2 * 4])
            push(s, CHUNKS[ck][1], yu, y_up.at[6 * t + ck])
            push(s, CHUNKS[ck][1], yd, y_down.at[6 * t + ck])
            to_core(s, ck)

        def across(ck):
            s = at(xp, ck)
            take(ref, s, CHUNKS[ck][1], x_a.at[2 * t + ck // 2])
            push(s, CHUNKS[ck][1], yu, y_up.at[6 * t + 4 + ck // 2])
            push(s, CHUNKS[ck][1], yd, y_down.at[6 * t + 4 + ck // 2])
            to_core(s, ck)

        def along(ck, partner):
            n = 6 * t + (4 + ck // 2 if partner else ck)
            h = (CHUNKS[ck][1] + ck // 2) // 2
            s = at(xpd if partner else yd, ck)
            take(ref, s, CHUNKS[ck][1], y_up.at[n])
            push(s, h, yu, y_far.at[n])
            if ck % 2:
                push(s, CHUNKS[ck][1], xp, x_b.at[8 * t + ck // 2 * 4 + 1])
            to_core(s, ck)
            s = at(xpu if partner else yu, ck)
            take(ref, s, CHUNKS[ck][1], y_down.at[n])
            push(s + h, CHUNKS[ck][1] - h, yd, y_far.at[n])
            if ck % 2:
                push(s, CHUNKS[ck][1], xp, x_b.at[8 * t + ck // 2 * 4 + 2])
            to_core(s, ck)

        def far(ck, partner):
            n = 6 * t + (4 + ck // 2 if partner else ck)
            s = at(xpo if partner else yo, ck)
            take(ref, s, CHUNKS[ck][1], y_far.at[n])
            if ck % 2:
                push(s, CHUNKS[ck][1], xp, x_b.at[8 * t + ck // 2 * 4 + 3])
            to_core(s, ck)

        def beside(ck, n):
            s = at((xp, xpd, xpu, xpo)[n], ck)
            take(ref, s, CHUNKS[ck][1], x_b.at[8 * t + ck // 2 * 4 + n])
            to_core(s, ck)

        def finish():
            take(ref, 0, TILES * PLANE // 2, core_in.at[t])

        return begin, across, along, far, beside, finish

    def score(i):
        e, row = source(i)
        place = (blk + e * (2 - 4 * xl)) % per * TILES + row
        q = q_all[i]
        here = here_all[i]
        top = None
        for slot in range(width):
            block = rows[slot, place]
            column = (block + xh) % 2
            group, dz = block // TILES, (block % TILES // 2 - z + Z) % Z
            tile = (group + column * (2 - group // 2 % 2 * 4)) * TILES + column * Z + place_of(dz)
            tiles_of[i, slot] = tile
            raw = lax.dot_general(q, k_all[tile], (((1,), (1,)), ((), ())), preferred_element_type=jnp.float32)
            now = raw * SCALE2 - jnp.abs(here - frame_row[block].astype(jnp.float32) * slope)
            scores[:, slot * BLOCK : (slot + 1) * BLOCK] = now
            top = now if top is None else jnp.maximum(top, now)
        top_now[...] = jnp.broadcast_to(jnp.max(top, axis=1, keepdims=True), (BLOCK, BLOCK))

    def weigh(i):
        top = top_now[...]
        total = jnp.zeros((BLOCK, BLOCK), jnp.float32)
        for slot in range(width):
            w = jnp.exp2(scores[:, slot * BLOCK : (slot + 1) * BLOCK] - top)
            total = total + w
            w_all[i, :, slot * BLOCK : (slot + 1) * BLOCK] = w.astype(w_all.dtype)
        total_all[i] = total

    begin, across, along, far, beside, finish = gather(0, k_all)
    value_begin, value_across, value_along, value_far, value_beside, value_finish = gather(1, v_all)
    begin(0), begin(1)
    frame_copy.wait()
    pattern.wait()
    lax.fori_loop(0, TILES, query_frames, 0)
    across(0), along(0, False), begin(2), along(1, False), beside(1, 0), along(0, True)
    begin(3), across(2), far(0, False), far(1, False), along(2, False), beside(1, 1), beside(1, 2), far(0, True)
    along(3, False), beside(3, 0), along(2, True), beside(1, 3), far(2, False), far(3, False)
    value_begin(0), value_begin(1)
    beside(3, 1), beside(3, 2), far(2, True), beside(3, 3), finish()
    own[2].wait()
    take(q_all, 1, TILES - 1, q_in.at[0])
    value_begin(2), value_begin(3)
    later = {
        1: [lambda: value_across(0), lambda: value_along(0, False)],
        4: [lambda: value_along(1, False)],
        5: [lambda: value_beside(1, 0)],
        8: [lambda: value_across(2), lambda: value_along(2, False)],
        12: [lambda: value_along(3, False)],
        13: [lambda: value_beside(3, 0)],
        16: [lambda: value_along(0, True)],
        17: [lambda: value_beside(1, 1)],
        18: [lambda: value_far(0, False)],
        19: [lambda: value_far(1, False)],
        20: [lambda: value_beside(1, 2)],
        23: [lambda: value_along(2, True)],
        24: [lambda: value_beside(3, 1)],
        25: [lambda: value_far(2, False)],
    }

    def pass_on(i, part):
        for half, steps in later.items():
            if half % 2 == part:

                @pl.when(i == half // 2)
                def _(steps=steps):
                    for step in steps:
                        step()

    def weigh_and_pass(j, carry):
        i = TILES - 1 - j
        score(i)
        pass_on(j, 0)
        weigh(i)
        pass_on(j, 1)
        return carry

    lax.fori_loop(0, TILES - LATE, weigh_and_pass, 0)
    value_far(3, False), value_beside(3, 2), value_far(0, True), value_far(2, True), value_beside(1, 3)
    value_beside(3, 3), value_finish()

    def home(i):
        e, dz = i // Z, offset_at(i % Z)
        to = ((z + dz) % Z) * 2 + (xh + e) % 2
        return (blk + e * (2 - 4 * xl), to)

    def block_row(j, carry):
        i = TILES - 1 - j

        @pl.when(i < LATE)
        def _():
            score(i)
            weigh(i)

        acc = jnp.zeros((BLOCK, HD), jnp.float32)
        for slot in range(0, width, 2):
            both = jnp.concatenate([v_all[tiles_of[i, slot]], v_all[tiles_of[i, slot + 1]]], axis=0)
            acc = acc + jnp.dot(
                w_all[i, :, slot * BLOCK : (slot + 2) * BLOCK], both, preferred_element_type=jnp.float32
            )
        o_all[i] = (acc / jnp.sum(total_all[i], axis=1, keepdims=True)).astype(o_all.dtype)

        @pl.when(i > 0)
        def _():
            pltpu.make_async_remote_copy(
                o_all.at[i], head_tile(out, head), o_send.at[0], o_in.at[0], device_id=home(i), device_id_type=MESH
            ).start()

        return carry

    lax.fori_loop(0, TILES, block_row, 0)
    last = pltpu.make_async_copy(o_all.at[0], head_tile(out, head), local.at[3])
    last.start()
    last.wait()
    take(o_all, 1, TILES - 1, o_in.at[0])
    take(o_all, 1, TILES - 1, o_send.at[0])
    take(q_all, 1, TILES - 1, send.at[2])
    for t, ref in ((0, k_all), (1, v_all)):
        take(ref, 0, 15 + 128 + (64 - 3 * CROSS_FIRST) + (48 + 3 * CROSS_FIRST), send.at[t])


def per_device(queries, keys, values, slopes, frames, block_list):
    blocks, width = block_list.shape[1:]
    smem = pl.BlockSpec(memory_space=pltpu.SMEM)
    hbm = pl.BlockSpec(memory_space=pl.ANY)
    dma = pltpu.SemaphoreType.DMA
    return pl.pallas_call(
        functools.partial(kernel, width),
        out_shape=jax.ShapeDtypeStruct(queries.shape, jnp.bfloat16),
        in_specs=[smem, hbm, hbm, hbm, hbm, hbm],
        out_specs=hbm,
        scratch_shapes=[
            pltpu.SMEM((width, LANES), jnp.int32),
            pltpu.SMEM((TILES, width), jnp.int32),
            pltpu.VMEM((blocks, 1, BLOCK), jnp.int32),
            pltpu.VMEM((TILES, BLOCK, BLOCK), jnp.float32),
            pltpu.VMEM((TILES, BLOCK, HD), jnp.bfloat16),
            pltpu.VMEM((blocks, BLOCK, HD), jnp.bfloat16),
            pltpu.VMEM((blocks, BLOCK, HD), jnp.bfloat16),
            pltpu.VMEM((TILES, BLOCK, HD), jnp.bfloat16),
            pltpu.VMEM((BLOCK, width * BLOCK), jnp.float32),
            pltpu.VMEM((BLOCK, BLOCK), jnp.float32),
            pltpu.VMEM((TILES, BLOCK, width * BLOCK), jnp.bfloat16),
            pltpu.VMEM((TILES, BLOCK, BLOCK), jnp.float32),
            dma((6,)), dma((3,)), dma((8,)), dma((4,)), dma((16,)), dma((12,)), dma((12,)), dma((12,)),
            dma((2,)), dma((1,)), dma((1,)), dma((1,)),
        ],
        compiler_params=pltpu.CompilerParams(collective_id=0, has_side_effects=True, vmem_limit_bytes=56 << 20),
    )(slopes, block_list.transpose(0, 2, 1), queries, keys, values, frames.reshape(blocks, 1, BLOCK))


def solution(mesh):
    rows = P(("blk", "head"), None)
    return jax.shard_map(
        per_device, mesh=mesh, in_specs=(rows, rows, rows, P(), P(), P()), out_specs=rows, check_vma=False
    )
```
